32 devices in a mesh: fsdp: 4 (over y, x), ctx: 8 (over z, core).
Axes of the slice: x: 2, y: 2, z: 4, core: 2. Of those that a mesh axis runs over, the one named last changes fastest.
Arguments:
- tokens: bfloat16 [4, 1024, 5376], P('fsdp', 'ctx'), may hold values from -6 to 6
- pre_gain: float32 [5376], replicated, may hold values from 0.1 to 1.9
- w_query: bfloat16 [5376, 3072], P(None, 'fsdp'), may hold values from -0.078125 to 0.078125
- key_weight: bfloat16 [5376, 1536], P(None, 'fsdp'), may hold values from -0.078125 to 0.078125
- value_weight: bfloat16 [5376, 1536], P(None, 'fsdp'), may hold values from -0.078125 to 0.078125
- query_norm_gain: float32 [128], replicated, may hold values from 0.1 to 1.9
- key_gain: float32 [128], replicated, may hold values from 0.1 to 1.9
- w_out: bfloat16 [3072, 5376], P('fsdp'), may hold values from -0.109375 to 0.109375
- post_gain: float32 [5376], replicated, may hold values from 0.1 to 1.9
Outputs:
- layer_out: bfloat16 [4, 1024, 5376], P('fsdp', 'ctx')
The draws below stay inside these ranges and needn't reach their ends.
All inputs are finite; a program needn't handle non-finite values.
Results may differ from the reference program's by a relative error of at most 0.012.
Values may be sent and summed in bfloat16 or wider, within the bound.
A program may use at most 128 MiB of HBM per device.

```python
import jax
import jax.numpy as jnp
from jax import lax

MODEL_WIDTH = 5376
QUERY_HEADS = 24
KEY_VALUE_HEADS = 12
HEAD_SIZE = 128
WINDOW = 1024
LEN = 1024
DOCS = 4
N_FSDP = 4


def level_of(key, dims, shards, least, top_value):
    level, own = 1.0, jax.random.fold_in(key, 6)
    for axis_at, shards_of in shards:
        heights = jnp.exp(jax.random.uniform(jax.random.fold_in(own, axis_at), (shards_of,), jnp.float32, least / len(shards), top_value / len(shards)))
        level = level * jnp.repeat(heights, dims[axis_at] // shards_of).reshape([-1 if axis == axis_at else 1 for axis in range(len(dims))])
    return level


def gaussian(stream_key, extent, scale, reach, split=(), held_as=jnp.bfloat16):
    values = jax.random.normal(stream_key, extent, jnp.float32) * scale
    if len(split) > 0:
        values = level_of(stream_key, extent, split, -0.22, 0.18) * values
    return jnp.clip(values, min=-reach, max=reach).astype(held_as)


def setup_inputs(seed: int = 0) -> dict:
    splits = jax.random.split(jax.random.key(seed), 10)
    tokens = gaussian(splits[0], (DOCS, LEN, MODEL_WIDTH), 1.0, 6.0, ((0, 4), (1, 8)))
    pre_gain = jnp.clip(1.0 + 0.18 * jax.random.normal(splits[1], (MODEL_WIDTH,), jnp.float32), 0.1, 1.9)
    w_query = gaussian(splits[2], (MODEL_WIDTH, QUERY_HEADS * HEAD_SIZE), MODEL_WIDTH ** -0.5, 0.078125, ((1, 4),))
    key_weight = gaussian(splits[3], (MODEL_WIDTH, KEY_VALUE_HEADS * HEAD_SIZE), MODEL_WIDTH ** -0.5, 0.078125, ((1, 4),))
    value_weight = gaussian(splits[4], (MODEL_WIDTH, KEY_VALUE_HEADS * HEAD_SIZE), MODEL_WIDTH ** -0.5, 0.078125, ((1, 4),))
    query_norm_gain = jnp.clip(1.0 + 0.18 * jax.random.normal(splits[5], (HEAD_SIZE,), jnp.float32), 0.1, 1.9)
    key_gain = jnp.clip(1.0 + 0.18 * jax.random.normal(splits[6], (HEAD_SIZE,), jnp.float32), 0.1, 1.9)
    w_out = gaussian(splits[7], (QUERY_HEADS * HEAD_SIZE, MODEL_WIDTH), (QUERY_HEADS * HEAD_SIZE) ** -0.5, 0.109375, ((0, 4),))
    post_gain = jnp.clip(1.0 + 0.18 * jax.random.normal(splits[8], (MODEL_WIDTH,), jnp.float32), 0.1, 1.9)
    return dict(tokens=tokens, pre_gain=pre_gain, w_query=w_query, key_weight=key_weight, value_weight=value_weight, query_norm_gain=query_norm_gain, key_gain=key_gain, w_out=w_out, post_gain=post_gain)


epsilon = 1e-06
score_scale = 168.0 ** (-0.5)

def root_mean_norm(values, gain):
    mean_sq = lax.optimization_barrier(jnp.mean(values * values, axis=-1, keepdims=True))
    return values * lax.rsqrt(mean_sq + epsilon) * gain

def rotary_embed(values, token_positions):
    half_dim = values.shape[-1] // 2
    frequencies = 10000.0 ** (-jnp.arange(half_dim, dtype=jnp.float32) / half_dim)
    angles = token_positions.astype(jnp.float32)[:, None] * frequencies[None, :]
    cosine = jnp.cos(angles)[:, None, :]
    sine_part = jnp.sin(angles)[:, None, :]
    first_half = values[..., :half_dim]
    second_half = values[..., half_dim:]
    return jnp.concatenate([first_half * cosine - second_half * sine_part, second_half * cosine + first_half * sine_part], axis=-1)

def stored_rows(values):
    return lax.optimization_barrier(values.astype(jnp.bfloat16)).astype(jnp.float32)

def reference(tokens, pre_gain, w_query, key_weight, value_weight, query_norm_gain, key_gain, w_out, post_gain):
    query_group_size = QUERY_HEADS // KEY_VALUE_HEADS
    group_cols = QUERY_HEADS * HEAD_SIZE // N_FSDP

    def one_document(doc_tokens):
        document_length = doc_tokens.shape[0]
        token_positions = jnp.arange(document_length, dtype=jnp.int32)
        normalized_rows = root_mean_norm(doc_tokens.astype(jnp.float32), pre_gain).astype(jnp.bfloat16)
        query_rows = jnp.dot(normalized_rows, w_query, preferred_element_type=jnp.float32).reshape(document_length, QUERY_HEADS, HEAD_SIZE)
        key_portion = jnp.dot(normalized_rows, key_weight, preferred_element_type=jnp.float32).reshape(document_length, KEY_VALUE_HEADS, HEAD_SIZE)
        value_portion = jnp.dot(normalized_rows, value_weight, preferred_element_type=jnp.float32).reshape(document_length, KEY_VALUE_HEADS, HEAD_SIZE)
        query_rows = stored_rows(rotary_embed(root_mean_norm(query_rows, query_norm_gain), token_positions)).reshape(document_length, KEY_VALUE_HEADS, query_group_size, HEAD_SIZE)
        key_portion = stored_rows(rotary_embed(root_mean_norm(key_portion, key_gain), token_positions))
        value_portion = stored_rows(value_portion)
        allowed = (token_positions[None, :] <= token_positions[:, None]) & (token_positions[:, None] - token_positions[None, :] < WINDOW)

        def single_head(head_index):
            q_head = query_rows[:, head_index]
            k_head = key_portion[:, head_index]
            v_head = value_portion[:, head_index]
            scores = jnp.einsum('qgc,kc->gqk', q_head, k_head) * score_scale
            unnorm = jnp.where(allowed[None], jnp.exp(scores), 0.0)
            totals = lax.optimization_barrier(jnp.sum(unnorm, axis=-1, keepdims=True))
            weights = stored_rows(unnorm / totals)
            return jnp.einsum('gqk,kc->qgc', weights, v_head).astype(jnp.bfloat16)
        head_outputs = lax.map(single_head, jnp.arange(KEY_VALUE_HEADS, dtype=jnp.int32))
        attended = jnp.transpose(head_outputs, (1, 0, 2, 3)).reshape(document_length, QUERY_HEADS * HEAD_SIZE)
        summed = jnp.zeros((document_length, MODEL_WIDTH), jnp.float32)
        for group_part in range(N_FSDP):
            lower = group_part * group_cols
            product = jnp.dot(attended[:, lower:lower + group_cols], w_out[lower:lower + group_cols], preferred_element_type=jnp.float32)
            summed = summed + stored_rows(product)
        return (doc_tokens.astype(jnp.float32) + root_mean_norm(summed, post_gain)).astype(jnp.bfloat16)
    return lax.map(one_document, tokens)
```

```python
import functools
import math

import jax
import jax.numpy as jnp
from jax import lax
from jax.experimental import pallas as pl
from jax.experimental.pallas import tpu as pltpu
from jax.sharding import PartitionSpec as P

epsilon = 1e-06
score_scale = 168.0 ** (-0.5)
window = 1024
MESH = pl.DeviceIdType.MESH
halves_of = ((0, 0), (1, 2), (2, 1), (3, 3))


def column_step(total, limit):
    step = 128
    for count in range(1, limit // 128 + 1):
        if total % (count * 128) == 0:
            step = count * 128
    return step


def layer_kernel(
    n_ctx, reach, q_heads, kv_heads, head,
    tok_hbm, wq_hbm, wk_hbm, wv_hbm, wo_hbm, pre_ref, post_ref, qg_ref, kg_ref, cos_ref, sin_ref,
    out_ref,
    tok, w, wo, nb, raw, q, kv, att, pb, rx, ry, dg,
    load_sem, ag_s, ag_r, rs_s, rs_r, z_s, z_r, b_s, b_r,
):
    f = lax.axis_index("fsdp")
    c = lax.axis_index("ctx")
    rows, features = tok.shape
    half = rows // 2
    z = c // 2
    p = c % 2
    nz = n_ctx // 2
    x_to = {"fsdp": f + 1 - 2 * (f % 2)}
    y_to = {"fsdp": (f + 2) % 4}
    sib = {"ctx": c + 1 - 2 * p}
    nxt = {"ctx": lax.rem(c + 2, n_ctx)}
    prv = {"ctx": lax.rem(c + n_ctx - 2, n_ctx)}
    has_next = z + 1 < nz
    has_prev = z > 0
    qw, kw = q_heads * head, kv_heads * head
    group = q_heads // kv_heads

    def load(i, src, dst):
        return pltpu.make_async_copy(src, dst, load_sem.at[i])

    loads = [load(0, tok_hbm, tok)]
    cut = features // 2
    for j, (src, lo, wide) in enumerate(((wk_hbm, qw, kw), (wv_hbm, qw + kw, kw), (wq_hbm, 0, qw))):
        for part in range(2):
            rs = pl.ds(part * cut, cut)
            loads.append(load(1 + 2 * j + part, src.at[rs], w.at[rs, pl.ds(lo, wide)]))
    wo_load = load(7, wo_hbm, wo)
    for d in loads:
        d.start()
    wo_load.start()

    barrier = pltpu.get_barrier_semaphore()
    for to in (x_to, y_to, sib):
        pl.semaphore_signal(barrier, inc=1, device_id=to, device_id_type=MESH)

    @pl.when(has_next)
    def _():
        pl.semaphore_signal(barrier, inc=1, device_id=nxt, device_id_type=MESH)

    @pl.when(has_prev)
    def _():
        pl.semaphore_signal(barrier, inc=1, device_id=prv, device_id_type=MESH)

    loads[0].wait()

    def norm_rows(i, carry):
        at = pl.ds(pl.multiple_of(i * 16, 16), 16)
        v = tok[at, :].astype(jnp.float32)
        mean_sq = jnp.mean(v * v, axis=-1, keepdims=True)
        nb[0, at, :] = (v * lax.rsqrt(mean_sq + epsilon) * pre_ref[...]).astype(jnp.bfloat16)
        return carry

    lax.fori_loop(0, rows // 16, norm_rows, 0)
    pl.semaphore_wait(barrier, 3 + jnp.minimum(z, 1) + jnp.minimum(nz - 1 - z, 1))

    A, B = pl.ds(0, half), pl.ds(half, half)

    def remote(src, dst, s, r, to):
        return pltpu.make_async_remote_copy(
            src_ref=src, dst_ref=dst, send_sem=s, recv_sem=r, device_id=to, device_id_type=MESH
        )

    def ag(i):
        src, dst, to = (
            (nb.at[0, A], nb.at[1, A], x_to),
            (nb.at[0, B], nb.at[2, B], x_to),
            (nb.at[0, B], nb.at[1, B], y_to),
            (nb.at[0, A], nb.at[2, A], y_to),
            (nb.at[1, A], nb.at[3, A], y_to),
            (nb.at[1, B], nb.at[3, B], x_to),
        )[i]
        return remote(src, dst, ag_s.at[i], ag_r.at[i], to)

    for i in (0, 2, 1, 3):
        ag(i).start()

    def z_copy(u, dz):
        return remote(kv.at[u, dz, p], kv.at[u, dz + 1, p], z_s.at[u, dz], z_r.at[u, dz + 1], nxt)

    def b_copy(u, dz):
        return remote(kv.at[u, dz, p], kv.at[u, dz, p], b_s.at[u, dz], b_r.at[u, dz], sib)

    def kv_arrived(u, dz):
        return remote(kv.at[u, dz, p], kv.at[u, dz, p], z_s.at[u, dz], z_r.at[u, dz], prv)

    def kv_paired(u, dz):
        return remote(kv.at[u, dz, 1 - p], kv.at[u, dz, 1 - p], b_s.at[u, dz], b_r.at[u, dz], sib)

    def send_own(u):
        @pl.when(has_next)
        def _():
            z_copy(u, 0).start()

        @pl.when(p == 0)
        def _():
            b_copy(u, 0).start()

    def relay(u, dz):
        if dz > reach:
            return

        @pl.when(z >= dz)
        def _():
            kv_arrived(u, dz).wait_recv()
            if dz < reach:
                @pl.when(has_next)
                def _():
                    z_copy(u, dz).start()
            b_copy(u, dz).start()

    def wait_pairs(u):
        @pl.when(p == 1)
        def _():
            kv_paired(u, 0).wait_recv()

        for dz in range(1, reach + 1):
            @pl.when(z >= dz)
            def _():
                kv_paired(u, dz).wait_recv()

    n_step = column_step(qw + 2 * kw, 256)

    def project(u):
        def columns(j, carry):
            at = pl.ds(pl.multiple_of(j * n_step, n_step), n_step)
            raw[:, at] = jnp.dot(nb[u], w[:, at], preferred_element_type=jnp.float32)
            return carry

        lax.fori_loop(0, (qw + 2 * kw) // n_step, columns, 0)

        def rotated(col, gain):
            v = raw[:, col : col + head]
            mean_sq = jnp.mean(v * v, axis=-1, keepdims=True)
            v = v * lax.rsqrt(mean_sq + epsilon) * gain[...]
            return (v * cos_ref[...] + pltpu.roll(v, head // 2, 1) * sin_ref[...]).astype(jnp.bfloat16)

        for h in range(kv_heads):
            kv[u, 0, p, :, h * head : (h + 1) * head] = rotated(qw + h * head, kg_ref)
        kv[u, 0, p, :, kw:] = raw[:, qw + kw :].astype(jnp.bfloat16)
        send_own(u)
        for h in range(q_heads):
            q[u, :, h * head : (h + 1) * head] = rotated(h * head, qg_ref)

    def attend(r):
        ua, ub = halves_of[r]

        def merged(first, second):
            return jnp.concatenate([first, second], axis=0)

        for g in range(kv_heads):
            kc = slice(g * head, (g + 1) * head)
            vc = slice(kw + g * head, kw + (g + 1) * head)

            def block(dz, par, cols):
                if ua == ub:
                    return kv[ua, dz, par, :, cols]
                return merged(kv[ua, dz, par, :half, cols], kv[ub, dz, par, half:, cols])

            parts = []
            for h in range(g * group, (g + 1) * group):
                hc = slice(h * head, (h + 1) * head)
                parts += [q[ua, :half, hc], q[ub, half:, hc]]
            qs = jnp.concatenate(parts, axis=0)

            def expo_of(keys):
                s = lax.dot_general(qs, keys, (((1,), (1,)), ((), ())), preferred_element_type=jnp.float32)
                return jnp.exp(s * score_scale)

            def times(e, values):
                return jnp.dot(e.astype(jnp.bfloat16), values, preferred_element_type=jnp.float32)

            qi = lax.broadcasted_iota(jnp.int32, (group, rows, rows), 1).reshape(group * rows, rows)
            kj = lax.broadcasted_iota(jnp.int32, (group * rows, rows), 1)
            e = jnp.where(kj <= qi, expo_of(block(0, p, kc)), 0.0)
            total, acc = e, times(e, block(0, p, vc))

            def beside(_, carry):
                total, acc = carry
                e = expo_of(block(0, 0, kc))
                return total + e, acc + times(e, block(0, 0, vc))

            def earlier(dz, carry):
                total, acc = carry
                e = expo_of(merged(block(dz, 0, kc), block(dz, 1, kc)))
                if n_ctx * rows > window:
                    apart = (p + 2 * dz) * rows + qi - kj
                    e = jnp.where(jnp.concatenate([apart, apart - rows], axis=1) < window, e, 0.0)
                acc = acc + times(e, merged(block(dz, 0, vc), block(dz, 1, vc)))
                return total + e[:, :rows] + e[:, rows:], acc

            total, acc = lax.fori_loop(0, p, beside, (total, acc))
            total, acc = lax.fori_loop(1, jnp.minimum(z, reach) + 1, earlier, (total, acc))
            o = (acc / jnp.sum(total, axis=-1, keepdims=True)).astype(jnp.bfloat16)
            for i in range(group):
                h = g * group + i
                hc = slice(h * head, (h + 1) * head)
                att[ua, :half, hc] = o[i * rows : i * rows + half]
                att[ub, half:, hc] = o[i * rows + half : (i + 1) * rows]

    o_step = column_step(features, 768)

    def output(u):
        def columns(j, carry):
            at = pl.ds(pl.multiple_of(j * o_step, o_step), o_step)
            pb[u, :, at] = jnp.dot(att[u], wo[:, at], preferred_element_type=jnp.float32).astype(jnp.bfloat16)
            return carry

        lax.fori_loop(0, features // o_step, columns, 0)

    quarter = half // 2
    A0, A1 = pl.ds(0, quarter), pl.ds(quarter, quarter)
    B0, B1 = pl.ds(half, quarter), pl.ds(half + quarter, quarter)

    def rs(i):
        src, dst, to = (
            (pb.at[1, A], rx.at[A], x_to),
            (pb.at[1, B], ry.at[B], y_to),
            (pb.at[3, A0], dg.at[A0], x_to),
            (pb.at[3, B0], dg.at[B0], y_to),
            (pb.at[3, A1], dg.at[A1], x_to),
            (pb.at[3, B1], dg.at[B1], y_to),
            (pb.at[2, A0], ry.at[A0], y_to),
            (pb.at[2, B0], rx.at[B0], x_to),
            (pb.at[2, A1], ry.at[A1], y_to),
            (pb.at[2, B1], rx.at[B1], x_to),
        )[i]
        return remote(src, dst, rs_s.at[i], rs_r.at[i], to)

    for d in loads[1:]:
        d.wait()
    project(0)
    ag(0).wait_recv()
    ag(4).start()
    ag(2).wait_recv()
    ag(5).start()
    relay(0, 1)
    project(1)
    relay(0, 2)
    relay(0, 3)
    relay(0, 4)
    relay(1, 1)
    wait_pairs(0)
    attend(0)
    wo_load.wait()
    output(0)
    relay(1, 2)
    ag(1).wait_recv()
    ag(3).wait_recv()
    project(2)
    relay(1, 3)
    relay(1, 4)
    relay(2, 1)
    ag(4).wait_recv()
    ag(5).wait_recv()
    project(3)
    relay(2, 2)
    relay(2, 3)
    relay(2, 4)
    relay(3, 1)
    wait_pairs(1)
    wait_pairs(2)
    attend(1)
    relay(3, 2)
    attend(2)
    output(1)
    rs(0).start()
    rs(1).start()
    relay(3, 3)
    relay(3, 4)
    wait_pairs(3)
    attend(3)
    output(3)
    for i in (2, 3, 4, 5):
        rs(i).start()
    output(2)

    def add_rows(first, count):
        def body(i, carry):
            at = pl.ds(pl.multiple_of(first + i * 16, 16), 16)
            pb[2, at, :] = (pb[2, at, :].astype(jnp.float32) + dg[at, :].astype(jnp.float32)).astype(jnp.bfloat16)
            return carry

        lax.fori_loop(0, count // 16, body, 0)

    for i, first in ((2, 0), (3, half), (4, quarter), (5, half + quarter)):
        rs(i).wait_recv()
        add_rows(first, quarter)
        rs(i + 4).start()

    def finish(first, count):
        def body(i, carry):
            at = pl.ds(pl.multiple_of(first + i * 16, 16), 16)
            summed = pb[0, at, :].astype(jnp.float32) + rx[at, :].astype(jnp.float32) + ry[at, :].astype(jnp.float32)
            mean_sq = jnp.mean(summed * summed, axis=-1, keepdims=True)
            normed = summed * lax.rsqrt(mean_sq + epsilon) * post_ref[...]
            out_ref[at, :] = (tok[at, :].astype(jnp.float32) + normed).astype(jnp.bfloat16)
            return carry

        lax.fori_loop(0, count // 16, body, 0)

    rs(0).wait_recv()
    rs(1).wait_recv()
    for i, first in ((6, 0), (7, half), (8, quarter), (9, half + quarter)):
        rs(i).wait_recv()
        finish(first, quarter)

    for i in range(6):
        ag(i).wait_send()
    for i in range(10):
        rs(i).wait_send()
    for u in range(4):
        @pl.when(has_next)
        def _():
            z_copy(u, 0).wait_send()

        @pl.when(p == 0)
        def _():
            b_copy(u, 0).wait_send()

        for dz in range(1, reach + 1):
            @pl.when(z >= dz)
            def _():
                if dz < reach:
                    @pl.when(has_next)
                    def _():
                        z_copy(u, dz).wait_send()
                b_copy(u, dz).wait_send()


def per_device(
    n_ctx, tokens, pre_gain, w_query, key_weight, value_weight, query_norm_gain, key_gain, w_out, post_gain
):
    _, rows, features = tokens.shape
    head = query_norm_gain.shape[0]
    qw, kw = w_query.shape[1], key_weight.shape[1]
    reach = min(n_ctx // 2 - 1, -(-window // (2 * rows)))
    half_dim = head // 2
    positions = lax.axis_index("ctx") * rows + jnp.arange(rows, dtype=jnp.int32)
    frequencies = 10000.0 ** (-jnp.arange(half_dim, dtype=jnp.float32) / half_dim)
    angles = positions.astype(jnp.float32)[:, None] * frequencies[None, :]
    cosine, sine = jnp.cos(angles), jnp.sin(angles)
    cos_all = jnp.concatenate([cosine, cosine], axis=1)
    sin_all = jnp.concatenate([-sine, sine], axis=1)
    any_spec = pl.BlockSpec(memory_space=pl.ANY)
    vmem_spec = pl.BlockSpec(memory_space=pltpu.VMEM)
    bf16 = jnp.bfloat16
    dma = pltpu.SemaphoreType.DMA
    out = pl.pallas_call(
        functools.partial(layer_kernel, n_ctx, reach, qw // head, kw // head, head),
        out_shape=jax.ShapeDtypeStruct((rows, features), bf16),
        in_specs=[any_spec] * 5 + [vmem_spec] * 6,
        out_specs=vmem_spec,
        scratch_shapes=[
            pltpu.VMEM((rows, features), bf16),
            pltpu.VMEM((features, qw + 2 * kw), bf16),
            pltpu.VMEM((qw, features), bf16),
            pltpu.VMEM((4, rows, features), bf16),
            pltpu.VMEM((rows, qw + 2 * kw), jnp.float32),
            pltpu.VMEM((4, rows, qw), bf16),
            pltpu.VMEM((4, reach + 1, 2, rows, 2 * kw), bf16),
            pltpu.VMEM((4, rows, qw), bf16),
            pltpu.VMEM((4, rows, features), bf16),
            pltpu.VMEM((rows, features), bf16),
            pltpu.VMEM((rows, features), bf16),
            pltpu.VMEM((rows, features), bf16),
            dma((8,)), dma((6,)), dma((6,)), dma((10,)), dma((10,)),
            dma((4, reach + 1)), dma((4, reach + 1)), dma((4, reach + 1)), dma((4, reach + 1)),
        ],
        compiler_params=pltpu.CompilerParams(
            collective_id=0, has_side_effects=True, vmem_limit_bytes=66_000_000
        ),
    )(
        tokens[0], w_query, key_weight, value_weight, w_out,
        pre_gain[None], post_gain[None], query_norm_gain[None], key_gain[None], cos_all, sin_all,
    )
    return out[None]


def solution(mesh):
    return jax.shard_map(
        functools.partial(per_device, mesh.shape["ctx"]),
        mesh=mesh,
        in_specs=(
            P("fsdp", "ctx", None),
            P(),
            P(None, "fsdp"),
            P(None, "fsdp"),
            P(None, "fsdp"),
            P(),
            P(),
            P("fsdp", None),
            P(),
        ),
        out_specs=P("fsdp", "ctx", None),
        check_vma=False,
    )
```

```python
import functools
import math

import jax
import jax.numpy as jnp
from jax import lax
from jax.experimental import pallas as pl
from jax.experimental.pallas import tpu as pltpu
from jax.sharding import PartitionSpec as P

epsilon = 1e-06
score_scale = 168.0 ** (-0.5)
window = 1024
MESH = pl.DeviceIdType.MESH
halves_of = ((0, 0), (1, 2), (2, 1), (3, 3))


def column_step(total, limit):
    step = 128
    for count in range(1, limit // 128 + 1):
        if total % (count * 128) == 0:
            step = count * 128
    return step


def layer_kernel(
    n_ctx, reach, q_heads, kv_heads, head,
    tok_hbm, wq_hbm, wk_hbm, wv_hbm, wo_hbm, pre_ref, post_ref, qg_ref, kg_ref, cos_ref, sin_ref,
    out_ref,
    tok, w, wo, nb, raw, q, kv, att, pb, rx, ry, dg, pre, post, accs, sums,
    load_sem, ag_s, ag_r, rs_s, rs_r, z_s, z_r, b_s, b_r,
):
    f = lax.axis_index("fsdp")
    c = lax.axis_index("ctx")
    rows, features = tok.shape
    half = rows // 2
    z = c // 2
    p = c % 2
    nz = n_ctx // 2
    x_to = {"fsdp": f + 1 - 2 * (f % 2)}
    y_to = {"fsdp": (f + 2) % 4}
    sib = {"ctx": c + 1 - 2 * p}

    def ahead(step):
        return {"ctx": lax.rem(c + 2 * step, n_ctx)}, z + step < nz

    def behind(step):
        return {"ctx": lax.rem(c + n_ctx - 2 * step, n_ctx)}, z >= step

    direct = [step for step in (1, 3) if step <= reach]
    qw, kw = q_heads * head, kv_heads * head
    group = q_heads // kv_heads

    def load(i, src, dst):
        return pltpu.make_async_copy(src, dst, load_sem.at[i])

    loads = [load(0, tok_hbm, tok)]
    cut = features // 2
    for j, (src, lo, wide) in enumerate(((wk_hbm, qw, kw), (wv_hbm, qw + kw, kw), (wq_hbm, 0, qw))):
        for part in range(2):
            rs = pl.ds(part * cut, cut)
            loads.append(load(1 + 2 * j + part, src.at[rs], w.at[rs, pl.ds(lo, wide)]))
    wo_load = load(7, wo_hbm, wo)
    for d in loads:
        d.start()
    wo_load.start()

    barrier = pltpu.get_barrier_semaphore()
    for to in (x_to, y_to, sib):
        pl.semaphore_signal(barrier, inc=1, device_id=to, device_id_type=MESH)

    peers = 3
    for step in direct:
        for to, there in (ahead(step), behind(step)):
            pl.when(there)(functools.partial(
                pl.semaphore_signal, barrier, inc=1, device_id=to, device_id_type=MESH
            ))
        peers = peers + jnp.clip(z - step + 1, 0, 1) + jnp.clip(nz - z - step, 0, 1)

    for wide, gain in ((pre, pre_ref), (post, post_ref)):
        wide[...] = jnp.concatenate([gain[k : k + 1, :] for k in range(gain.shape[0])], axis=1)
    loads[0].wait()

    def norm_rows(i, carry):
        at = pl.ds(pl.multiple_of(i * 16, 16), 16)
        v = tok[at, :].astype(jnp.float32)
        mean_sq = jnp.mean(v * v, axis=-1, keepdims=True)
        nb[0, at, :] = (v * lax.rsqrt(mean_sq + epsilon) * pre[...]).astype(jnp.bfloat16)
        return carry

    lax.fori_loop(0, half // 16, norm_rows, 0)
    pl.semaphore_wait(barrier, peers)

    A, B = pl.ds(0, half), pl.ds(half, half)

    def remote(src, dst, s, r, to):
        return pltpu.make_async_remote_copy(
            src_ref=src, dst_ref=dst, send_sem=s, recv_sem=r, device_id=to, device_id_type=MESH
        )

    def ag(i):
        src, dst, to = (
            (nb.at[0, A], nb.at[1, A], x_to),
            (nb.at[0, B], nb.at[2, B], x_to),
            (nb.at[0, B], nb.at[1, B], y_to),
            (nb.at[0, A], nb.at[2, A], y_to),
            (nb.at[1, A], nb.at[3, A], y_to),
            (nb.at[1, B], nb.at[3, B], x_to),
        )[i]
        return remote(src, dst, ag_s.at[i], ag_r.at[i], to)

    ag(0).start()
    lax.fori_loop(half // 16, rows // 16, norm_rows, 0)
    for i in (2, 1, 3):
        ag(i).start()

    def z_copy(u, dz, step):
        return remote(
            kv.at[u, dz, p], kv.at[u, dz + step, p], z_s.at[u, dz + step], z_r.at[u, dz + step], ahead(step)[0]
        )

    def b_copy(u, dz):
        return remote(kv.at[u, dz, p], kv.at[u, dz, p], b_s.at[u, dz], b_r.at[u, dz], sib)

    def kv_arrived(u, dz):
        return remote(kv.at[u, dz, p], kv.at[u, dz, p], z_s.at[u, dz], z_r.at[u, dz], behind(1)[0])

    def kv_paired(u, dz):
        return remote(kv.at[u, dz, 1 - p], kv.at[u, dz, 1 - p], b_s.at[u, dz], b_r.at[u, dz], sib)

    def own_copies(u, act):
        for step in direct:
            @pl.when(ahead(step)[1])
            def _():
                act(z_copy(u, 0, step))

        @pl.when(p == 0)
        def _():
            act(b_copy(u, 0))

    def send_own(u):
        own_copies(u, lambda d: d.start())

    def passed_copies(u, dz, act):
        if dz in direct and dz + 1 <= reach:
            @pl.when(ahead(1)[1])
            def _():
                act(z_copy(u, dz, 1))

        act(b_copy(u, dz))

    def relay(u, dz):
        if dz > reach:
            return

        @pl.when(z >= dz)
        def _():
            kv_arrived(u, dz).wait_recv()
            passed_copies(u, dz, lambda d: d.start())

    def wait_pairs(u):
        @pl.when(p == 1)
        def _():
            kv_paired(u, 0).wait_recv()

        for dz in range(1, reach + 1):
            @pl.when(z >= dz)
            def _():
                kv_paired(u, dz).wait_recv()

    k_step = column_step(2 * kw, 256)
    q_step = column_step(qw, 256)

    def columns_of(u, first, count, step):
        def columns(j, carry):
            at = pl.ds(pl.multiple_of(first + j * step, 128), step)
            raw[:, at] = jnp.dot(nb[u], w[:, at], preferred_element_type=jnp.float32)
            return carry

        lax.fori_loop(0, count // step, columns, 0)

    def rotated(col, gain):
        v = raw[:, col : col + head]
        mean_sq = jnp.mean(v * v, axis=-1, keepdims=True)
        v = v * lax.rsqrt(mean_sq + epsilon) * gain[...]
        return (v * cos_ref[...] + pltpu.roll(v, head // 2, 1) * sin_ref[...]).astype(jnp.bfloat16)

    def project_keys(u):
        columns_of(u, qw, 2 * kw, k_step)
        for h in range(kv_heads):
            kv[u, 0, p, :, h * head : (h + 1) * head] = rotated(qw + h * head, kg_ref)
        kv[u, 0, p, :, kw:] = raw[:, qw + kw :].astype(jnp.bfloat16)

    def project_queries(u):
        columns_of(u, 0, qw, q_step)
        for h in range(q_heads):
            q[u, :, h * head : (h + 1) * head] = rotated(h * head, qg_ref)

    def merged(parts):
        return jnp.concatenate(parts, axis=0)

    def attend(docs):
        qi = lax.broadcasted_iota(jnp.int32, (group, rows, rows), 1).reshape(group * rows, rows)
        kj = lax.broadcasted_iota(jnp.int32, (group * rows, rows), 1)
        streams = [(i * kv_heads + g, g, halves_of[r]) for i, r in enumerate(docs) for g in range(kv_heads)]

        def block(units, dz, par, cols):
            ua, ub = units
            if ua == ub:
                return kv[ua, dz, par, :, cols]
            return merged([kv[ua, dz, par, :half, cols], kv[ub, dz, par, half:, cols]])

        def step(dz, pars, mask, first=False):
            for n, g, (ua, ub) in streams:
                kc = slice(g * head, (g + 1) * head)
                vc = slice(kw + g * head, kw + (g + 1) * head)
                parts = []
                for h in range(g * group, (g + 1) * group):
                    hc = slice(h * head, (h + 1) * head)
                    parts += [q[ua, :half, hc], q[ub, half:, hc]]
                keys = merged([block((ua, ub), dz, par, kc) for par in pars])
                values = merged([block((ua, ub), dz, par, vc) for par in pars])
                s = lax.dot_general(
                    merged(parts), keys, (((1,), (1,)), ((), ())), preferred_element_type=jnp.float32
                )
                e = jnp.exp(s * score_scale)
                if mask is not None:
                    e = jnp.where(mask, e, 0.0)
                total = sum(e[:, i * rows : (i + 1) * rows] for i in range(len(pars)))
                acc = jnp.dot(e.astype(jnp.bfloat16), values, preferred_element_type=jnp.float32)
                if first:
                    sums[n], accs[n] = total, acc
                else:
                    sums[n] += total
                    accs[n] += acc

        step(0, [p], kj <= qi, True)

        def beside(_, carry):
            step(0, [0], None)
            return carry

        def earlier(dz, carry):
            mask = None
            if n_ctx * rows > window:
                apart = (p + 2 * dz) * rows + qi - kj
                mask = jnp.concatenate([apart, apart - rows], axis=1) < window
            step(dz, [0, 1], mask)
            return carry

        lax.fori_loop(0, p, beside, 0)
        lax.fori_loop(1, jnp.minimum(z, reach) + 1, earlier, 0)
        for n, g, (ua, ub) in streams:
            o = (accs[n] / jnp.sum(sums[n], axis=-1, keepdims=True)).astype(jnp.bfloat16)
            for i in range(group):
                h = g * group + i
                hc = slice(h * head, (h + 1) * head)
                att[ua, :half, hc] = o[i * rows : i * rows + half]
                att[ub, half:, hc] = o[i * rows + half : (i + 1) * rows]

    o_step = column_step(features, 768)

    def output(u):
        def columns(j, carry):
            at = pl.ds(pl.multiple_of(j * o_step, o_step), o_step)
            pb[u, :, at] = jnp.dot(att[u], wo[:, at], preferred_element_type=jnp.float32).astype(jnp.bfloat16)
            return carry

        lax.fori_loop(0, features // o_step, columns, 0)

    quarter = half // 2
    A0, A1 = pl.ds(0, quarter), pl.ds(quarter, quarter)
    B0, B1 = pl.ds(half, quarter), pl.ds(half + quarter, quarter)

    def rs(i):
        src, dst, to = (
            (pb.at[1, A], rx.at[A], x_to),
            (pb.at[1, B], ry.at[B], y_to),
            (pb.at[3, A0], dg.at[A0], x_to),
            (pb.at[3, B0], dg.at[B0], y_to),
            (pb.at[3, A1], dg.at[A1], x_to),
            (pb.at[3, B1], dg.at[B1], y_to),
            (pb.at[2, A0], ry.at[A0], y_to),
            (pb.at[2, B0], rx.at[B0], x_to),
            (pb.at[2, A1], ry.at[A1], y_to),
            (pb.at[2, B1], rx.at[B1], x_to),
        )[i]
        return remote(src, dst, rs_s.at[i], rs_r.at[i], to)

    for d in loads[1:]:
        d.wait()
    project_keys(0)
    ag(0).wait_recv()
    ag(4).start()
    ag(2).wait_recv()
    ag(5).start()
    project_keys(1)
    send_own(1)
    project_queries(1)
    relay(1, 1)
    project_queries(0)
    ag(1).wait_recv()
    ag(3).wait_recv()
    project_keys(2)
    send_own(2)
    for dz in range(2, reach + 1):
        relay(1, dz)
    project_queries(2)
    relay(2, 1)
    ag(4).wait_recv()
    ag(5).wait_recv()
    project_keys(3)
    send_own(3)
    send_own(0)
    for dz in range(2, reach + 1):
        relay(2, dz)
    wo_load.wait()
    wait_pairs(1)
    wait_pairs(2)
    attend((1, 2))
    relay(3, 1)
    output(1)
    rs(0).start()
    rs(1).start()
    project_queries(3)
    relay(0, 1)
    for dz in range(2, reach + 1):
        relay(3, dz)
    wait_pairs(3)
    attend((3,))
    output(3)
    for i in (2, 3, 4, 5):
        rs(i).start()
    output(2)
    for dz in range(2, reach + 1):
        relay(0, dz)
    wait_pairs(0)
    attend((0,))
    output(0)

    def add_rows(first, count):
        def body(i, carry):
            at = pl.ds(pl.multiple_of(first + i * 16, 16), 16)
            pb[2, at, :] = (pb[2, at, :].astype(jnp.float32) + dg[at, :].astype(jnp.float32)).astype(jnp.bfloat16)
            return carry

        lax.fori_loop(0, count // 16, body, 0)

    for i, first in ((2, 0), (3, half), (4, quarter), (5, half + quarter)):
        rs(i).wait_recv()
        add_rows(first, quarter)
        rs(i + 4).start()

    def finish(first, count):
        def body(i, carry):
            at = pl.ds(pl.multiple_of(first + i * 16, 16), 16)
            summed = pb[0, at, :].astype(jnp.float32) + rx[at, :].astype(jnp.float32) + ry[at, :].astype(jnp.float32)
            mean_sq = jnp.mean(summed * summed, axis=-1, keepdims=True)
            normed = summed * lax.rsqrt(mean_sq + epsilon) * post[...]
            out_ref[at, :] = (tok[at, :].astype(jnp.float32) + normed).astype(jnp.bfloat16)
            return carry

        lax.fori_loop(0, count // 16, body, 0)

    rs(0).wait_recv()
    rs(1).wait_recv()
    for i, first in ((6, 0), (7, half), (8, quarter), (9, half + quarter)):
        rs(i).wait_recv()
        finish(first, quarter)

    for i in range(6):
        ag(i).wait_send()
    for i in range(10):
        rs(i).wait_send()
    for u in range(4):
        own_copies(u, lambda d: d.wait_send())
        for dz in range(1, reach + 1):
            @pl.when(z >= dz)
            def _():
                passed_copies(u, dz, lambda d: d.wait_send())


def per_device(
    n_ctx, tokens, pre_gain, w_query, key_weight, value_weight, query_norm_gain, key_gain, w_out, post_gain
):
    _, rows, features = tokens.shape
    head = query_norm_gain.shape[0]
    qw, kw = w_query.shape[1], key_weight.shape[1]
    reach = min(n_ctx // 2 - 1, -(-window // (2 * rows)))
    half_dim = head // 2
    positions = lax.axis_index("ctx") * rows + jnp.arange(rows, dtype=jnp.int32)
    frequencies = 10000.0 ** (-jnp.arange(half_dim, dtype=jnp.float32) / half_dim)
    angles = positions.astype(jnp.float32)[:, None] * frequencies[None, :]
    cosine, sine = jnp.cos(angles), jnp.sin(angles)
    cos_all = jnp.concatenate([cosine, cosine], axis=1)
    sin_all = jnp.concatenate([-sine, sine], axis=1)
    any_spec = pl.BlockSpec(memory_space=pl.ANY)
    vmem_spec = pl.BlockSpec(memory_space=pltpu.VMEM)
    bf16 = jnp.bfloat16
    dma = pltpu.SemaphoreType.DMA
    out = pl.pallas_call(
        functools.partial(layer_kernel, n_ctx, reach, qw // head, kw // head, head),
        out_shape=jax.ShapeDtypeStruct((rows, features), bf16),
        in_specs=[any_spec] * 5 + [vmem_spec] * 6,
        out_specs=vmem_spec,
        scratch_shapes=[
            pltpu.VMEM((rows, features), bf16),
            pltpu.VMEM((features, qw + 2 * kw), bf16),
            pltpu.VMEM((qw, features), bf16),
            pltpu.VMEM((4, rows, features), bf16),
            pltpu.VMEM((rows, qw + 2 * kw), jnp.float32),
            pltpu.VMEM((4, rows, qw), bf16),
            pltpu.VMEM((4, reach + 1, 2, rows, 2 * kw), bf16),
            pltpu.VMEM((4, rows, qw), bf16),
            pltpu.VMEM((4, rows, features), bf16),
            pltpu.VMEM((rows, features), bf16),
            pltpu.VMEM((rows, features), bf16),
            pltpu.VMEM((rows, features), bf16),
            pltpu.VMEM((1, features), jnp.float32),
            pltpu.VMEM((1, features), jnp.float32),
            pltpu.VMEM((2 * kw // head, qw // kw * rows, head), jnp.float32),
            pltpu.VMEM((2 * kw // head, qw // kw * rows, rows), jnp.float32),
            dma((8,)), dma((6,)), dma((6,)), dma((10,)), dma((10,)),
            dma((4, reach + 1)), dma((4, reach + 1)), dma((4, reach + 1)), dma((4, reach + 1)),
        ],
        compiler_params=pltpu.CompilerParams(
            collective_id=0, has_side_effects=True, vmem_limit_bytes=66_000_000
        ),
    )(
        tokens[0], w_query, key_weight, value_weight, w_out,
        pre_gain.reshape(-1, 128), post_gain.reshape(-1, 128), query_norm_gain[None], key_gain[None], cos_all, sin_all,
    )
    return out[None]


def solution(mesh):
    return jax.shard_map(
        functools.partial(per_device, mesh.shape["ctx"]),
        mesh=mesh,
        in_specs=(
            P("fsdp", "ctx", None),
            P(),
            P(None, "fsdp"),
            P(None, "fsdp"),
            P(None, "fsdp"),
            P(),
            P(),
            P("fsdp", None),
            P(),
        ),
        out_specs=P("fsdp", "ctx", None),
        check_vma=False,
    )
```

```python
import functools
import math

import jax
import jax.numpy as jnp
from jax import lax
from jax.experimental import pallas as pl
from jax.experimental.pallas import tpu as pltpu
from jax.sharding import PartitionSpec as P

epsilon = 1e-06
score_scale = 168.0 ** (-0.5)
window = 1024
vmem_limit = 58_000_000
MESH = pl.DeviceIdType.MESH
halves_of = ((0, 0), (1, 2), (2, 1), (3, 3))


def column_step(total, limit):
    step = 128
    for count in range(1, limit // 128 + 1):
        if total % (count * 128) == 0:
            step = count * 128
    return step


def layer_kernel(
    n_ctx, reach, q_heads, kv_heads, head,
    tok_hbm, wq_hbm, wk_hbm, wv_hbm, wo_hbm, pre_ref, post_ref, qg_ref, kg_ref, cos_ref, sin_ref,
    out_ref,
    tok, w, wo, nb, raw, q, kv, att, pb, rx, ry, dg, pre, post, accs, sums,
    load_sem, ag_s, ag_r, rs_s, rs_r, z_s, z_r, b_s, b_r,
):
    f = lax.axis_index("fsdp")
    c = lax.axis_index("ctx")
    rows, features = tok.shape
    half = rows // 2
    z = c // 2
    p = c % 2
    nz = n_ctx // 2
    x_to = {"fsdp": f + 1 - 2 * (f % 2)}
    y_to = {"fsdp": (f + 2) % 4}
    sib = {"ctx": c + 1 - 2 * p}

    def ahead(step):
        return {"ctx": lax.rem(c + 2 * step, n_ctx)}, z + step < nz

    def behind(step):
        return {"ctx": lax.rem(c + n_ctx - 2 * step, n_ctx)}, z >= step

    direct = [step for step in (1, 3) if step <= reach]
    qw, kw = q_heads * head, kv_heads * head
    group = q_heads // kv_heads

    def load(i, src, dst):
        return pltpu.make_async_copy(src, dst, load_sem.at[i])

    tok_loads = [load(i, tok_hbm.at[pl.ds(i * half, half)], tok.at[pl.ds(i * half, half)]) for i in range(2)]
    for d in tok_loads:
        d.start()
    loads = []
    cut = features // 2
    for j, (src, lo, wide) in enumerate(((wk_hbm, qw, kw), (wv_hbm, qw + kw, kw), (wq_hbm, 0, qw))):
        for part in range(2):
            rs = pl.ds(part * cut, cut)
            loads.append(load(2 + 2 * j + part, src.at[rs], w.at[rs, pl.ds(lo, wide)]))
    wo_load = load(8, wo_hbm, wo)

    barrier = pltpu.get_barrier_semaphore()
    for to in (x_to, y_to, sib):
        pl.semaphore_signal(barrier, inc=1, device_id=to, device_id_type=MESH)

    peers = 3
    for step in direct:
        for to, there in (ahead(step), behind(step)):
            pl.when(there)(functools.partial(
                pl.semaphore_signal, barrier, inc=1, device_id=to, device_id_type=MESH
            ))
        peers = peers + jnp.clip(z - step + 1, 0, 1) + jnp.clip(nz - z - step, 0, 1)

    for wide, gain in ((pre, pre_ref), (post, post_ref)):
        wide[...] = jnp.concatenate([gain[k : k + 1, :] for k in range(gain.shape[0])], axis=1)
    tok_loads[0].wait()

    def norm_rows(i, carry):
        at = pl.ds(pl.multiple_of(i * 16, 16), 16)
        v = tok[at, :].astype(jnp.float32)
        mean_sq = jnp.mean(v * v, axis=-1, keepdims=True)
        nb[0, at, :] = (v * lax.rsqrt(mean_sq + epsilon) * pre[...]).astype(jnp.bfloat16)
        return carry

    lax.fori_loop(0, half // 16, norm_rows, 0)
    tok_loads[1].wait()
    for d in loads:
        d.start()
    wo_load.start()
    pl.semaphore_wait(barrier, peers)

    A, B = pl.ds(0, half), pl.ds(half, half)

    def remote(src, dst, s, r, to):
        return pltpu.make_async_remote_copy(
            src_ref=src, dst_ref=dst, send_sem=s, recv_sem=r, device_id=to, device_id_type=MESH
        )

    def ag(i):
        src, dst, to = (
            (nb.at[0, A], nb.at[1, A], x_to),
            (nb.at[0, B], nb.at[2, B], x_to),
            (nb.at[0, B], nb.at[1, B], y_to),
            (nb.at[0, A], nb.at[2, A], y_to),
            (nb.at[1, A], nb.at[3, A], y_to),
            (nb.at[1, B], nb.at[3, B], x_to),
        )[i]
        return remote(src, dst, ag_s.at[i], ag_r.at[i], to)

    ag(0).start()
    lax.fori_loop(half // 16, rows // 16, norm_rows, 0)
    for i in (2, 1, 3):
        ag(i).start()

    def z_copy(u, dz, step):
        return remote(
            kv.at[u, dz, p], kv.at[u, dz + step, p], z_s.at[u, dz + step], z_r.at[u, dz + step], ahead(step)[0]
        )

    def b_copy(u, dz):
        return remote(kv.at[u, dz, p], kv.at[u, dz, p], b_s.at[u, dz], b_r.at[u, dz], sib)

    def kv_arrived(u, dz):
        return remote(kv.at[u, dz, p], kv.at[u, dz, p], z_s.at[u, dz], z_r.at[u, dz], behind(1)[0])

    def kv_paired(u, dz):
        return remote(kv.at[u, dz, 1 - p], kv.at[u, dz, 1 - p], b_s.at[u, dz], b_r.at[u, dz], sib)

    def own_copies(u, act):
        for step in direct:
            @pl.when(ahead(step)[1])
            def _():
                act(z_copy(u, 0, step))

        @pl.when(p == 0)
        def _():
            act(b_copy(u, 0))

    def send_own(u):
        own_copies(u, lambda d: d.start())

    def passed_copies(u, dz, act):
        if dz in direct and dz + 1 <= reach:
            @pl.when(ahead(1)[1])
            def _():
                act(z_copy(u, dz, 1))

        act(b_copy(u, dz))

    def relay(u, dz):
        if dz > reach:
            return

        @pl.when(z >= dz)
        def _():
            kv_arrived(u, dz).wait_recv()
            passed_copies(u, dz, lambda d: d.start())

    def wait_pairs(u):
        @pl.when(p == 1)
        def _():
            kv_paired(u, 0).wait_recv()

        for dz in range(1, reach + 1):
            @pl.when(z >= dz)
            def _():
                kv_paired(u, dz).wait_recv()

    k_step = column_step(2 * kw, 256)
    q_step = column_step(qw, 256)

    def columns_of(u, first, count, step):
        def columns(j, carry):
            at = pl.ds(pl.multiple_of(first + j * step, 128), step)
            raw[:, at] = jnp.dot(nb[u], w[:, at], preferred_element_type=jnp.float32)
            return carry

        lax.fori_loop(0, count // step, columns, 0)

    def rotated(col, gain):
        v = raw[:, col : col + head]
        mean_sq = jnp.mean(v * v, axis=-1, keepdims=True)
        v = v * lax.rsqrt(mean_sq + epsilon) * gain[...]
        return (v * cos_ref[...] + pltpu.roll(v, head // 2, 1) * sin_ref[...]).astype(jnp.bfloat16)

    def project_keys(u):
        columns_of(u, qw, 2 * kw, k_step)
        for h in range(kv_heads):
            kv[u, 0, p, :, h * head : (h + 1) * head] = rotated(qw + h * head, kg_ref)
        kv[u, 0, p, :, kw:] = raw[:, qw + kw :].astype(jnp.bfloat16)

    def project_queries(u):
        columns_of(u, 0, qw, q_step)
        for h in range(q_heads):
            q[u, :, h * head : (h + 1) * head] = rotated(h * head, qg_ref)

    def merged(parts):
        return jnp.concatenate(parts, axis=0)

    def attend(u):
        own, other = halves_of[u], halves_of[(0, 2, 1, 3)[u]]
        spans = [(0, rows, own)] if own == other else [(0, half, own), (half, half, other)]
        streams = [
            (i * kv_heads + g, g, lo, size, units)
            for i, (lo, size, units) in enumerate(spans) for g in range(kv_heads)
        ]

        def places(lo, size):
            qi = lax.broadcasted_iota(jnp.int32, (group, size, rows), 1).reshape(group * size, rows) + lo
            return qi, lax.broadcasted_iota(jnp.int32, (group * size, rows), 1)

        def block(units, dz, par, cols):
            ua, ub = units
            if ua == ub:
                return kv[ua, dz, par, :, cols]
            return merged([kv[ua, dz, par, :half, cols], kv[ub, dz, par, half:, cols]])

        def step(dz, pars, mask, first=False):
            for n, g, lo, size, units in streams:
                kc = slice(g * head, (g + 1) * head)
                vc = slice(kw + g * head, kw + (g + 1) * head)
                at = slice(0, group * size)
                queries = merged([
                    q[u, lo : lo + size, h * head : (h + 1) * head] for h in range(g * group, (g + 1) * group)
                ])
                keys = merged([block(units, dz, par, kc) for par in pars])
                values = merged([block(units, dz, par, vc) for par in pars])
                s = lax.dot_general(queries, keys, (((1,), (1,)), ((), ())), preferred_element_type=jnp.float32)
                e = jnp.exp(s * score_scale)
                if mask is not None:
                    e = jnp.where(mask(lo, size), e, 0.0)
                total = sum(e[:, i * rows : (i + 1) * rows] for i in range(len(pars)))
                acc = jnp.dot(e.astype(jnp.bfloat16), values, preferred_element_type=jnp.float32)
                if first:
                    sums[n, at], accs[n, at] = total, acc
                else:
                    sums[n, at] += total
                    accs[n, at] += acc

        def causal(lo, size):
            qi, kj = places(lo, size)
            return kj <= qi

        step(0, [p], causal, True)

        def beside(_, carry):
            step(0, [0], None)
            return carry

        def earlier(dz, carry):
            def near(lo, size):
                qi, kj = places(lo, size)
                apart = (p + 2 * dz) * rows + qi - kj
                return jnp.concatenate([apart, apart - rows], axis=1) < window

            step(dz, [0, 1], near if n_ctx * rows > window else None)
            return carry

        lax.fori_loop(0, p, beside, 0)
        lax.fori_loop(1, jnp.minimum(z, reach) + 1, earlier, 0)
        for n, g, lo, size, _ in streams:
            at = slice(0, group * size)
            o = (accs[n, at] / jnp.sum(sums[n, at], axis=-1, keepdims=True)).astype(jnp.bfloat16)
            for i in range(group):
                h = g * group + i
                att[u, lo : lo + size, h * head : (h + 1) * head] = o[i * size : (i + 1) * size]

    o_step = column_step(features, 768)

    def output(u):
        def columns(j, carry):
            at = pl.ds(pl.multiple_of(j * o_step, o_step), o_step)
            pb[u, :, at] = jnp.dot(att[u], wo[:, at], preferred_element_type=jnp.float32).astype(jnp.bfloat16)
            return carry

        lax.fori_loop(0, features // o_step, columns, 0)

    quarter = half // 2
    A0, A1 = pl.ds(0, quarter), pl.ds(quarter, quarter)
    B0, B1 = pl.ds(half, quarter), pl.ds(half + quarter, quarter)

    def rs(i):
        src, dst, to = (
            (pb.at[1, A], rx.at[A], x_to),
            (pb.at[1, B], ry.at[B], y_to),
            (pb.at[3, A0], dg.at[A0], x_to),
            (pb.at[3, B0], dg.at[B0], y_to),
            (pb.at[3, A1], dg.at[A1], x_to),
            (pb.at[3, B1], dg.at[B1], y_to),
            (pb.at[2, A0], ry.at[A0], y_to),
            (pb.at[2, B0], rx.at[B0], x_to),
            (pb.at[2, A1], ry.at[A1], y_to),
            (pb.at[2, B1], rx.at[B1], x_to),
        )[i]
        return remote(src, dst, rs_s.at[i], rs_r.at[i], to)

    for d in loads:
        d.wait()
    project_keys(0)
    ag(0).wait_recv()
    ag(4).start()
    ag(2).wait_recv()
    ag(5).start()
    project_keys(1)
    send_own(1)
    project_queries(1)
    relay(1, 1)
    project_queries(0)
    ag(1).wait_recv()
    ag(3).wait_recv()
    project_keys(2)
    send_own(2)
    for dz in range(2, reach + 1):
        relay(1, dz)
    project_queries(2)
    relay(2, 1)
    ag(4).wait_recv()
    ag(5).wait_recv()
    project_keys(3)
    send_own(3)
    send_own(0)
    for dz in range(2, reach + 1):
        relay(2, dz)
    wo_load.wait()
    wait_pairs(1)
    wait_pairs(2)
    attend(1)
    output(1)
    rs(0).start()
    rs(1).start()
    relay(3, 1)
    attend(2)
    project_queries(3)
    relay(0, 1)
    for dz in range(2, reach + 1):
        relay(3, dz)
    wait_pairs(3)
    attend(3)
    output(3)
    for i in (2, 3, 4, 5):
        rs(i).start()
    output(2)

    def add_rows(first, count):
        def body(i, carry):
            at = pl.ds(pl.multiple_of(first + i * 16, 16), 16)
            pb[2, at, :] = (pb[2, at, :].astype(jnp.float32) + dg[at, :].astype(jnp.float32)).astype(jnp.bfloat16)
            return carry

        lax.fori_loop(0, count // 16, body, 0)

    for i, first in ((2, 0), (3, half), (4, quarter), (5, half + quarter)):
        rs(i).wait_recv()
        add_rows(first, quarter)
        rs(i + 4).start()
    for dz in range(2, reach + 1):
        relay(0, dz)
    wait_pairs(0)
    attend(0)
    output(0)

    def finish(first, count):
        def body(i, carry):
            at = pl.ds(pl.multiple_of(first + i * 16, 16), 16)
            summed = pb[0, at, :].astype(jnp.float32) + rx[at, :].astype(jnp.float32) + ry[at, :].astype(jnp.float32)
            mean_sq = jnp.mean(summed * summed, axis=-1, keepdims=True)
            normed = summed * lax.rsqrt(mean_sq + epsilon) * post[...]
            out_ref[at, :] = (tok[at, :].astype(jnp.float32) + normed).astype(jnp.bfloat16)
            return carry

        lax.fori_loop(0, count // 16, body, 0)

    rs(0).wait_recv()
    rs(1).wait_recv()
    for i, first in ((6, 0), (7, half), (8, quarter), (9, half + quarter)):
        rs(i).wait_recv()
        finish(first, quarter)

    for i in range(6):
        ag(i).wait_send()
    for i in range(10):
        rs(i).wait_send()
    for u in range(4):
        own_copies(u, lambda d: d.wait_send())
        for dz in range(1, reach + 1):
            @pl.when(z >= dz)
            def _():
                passed_copies(u, dz, lambda d: d.wait_send())


def per_device(
    n_ctx, tokens, pre_gain, w_query, key_weight, value_weight, query_norm_gain, key_gain, w_out, post_gain
):
    _, rows, features = tokens.shape
    head = query_norm_gain.shape[0]
    qw, kw = w_query.shape[1], key_weight.shape[1]
    reach = min(n_ctx // 2 - 1, -(-window // (2 * rows)))
    half_dim = head // 2
    positions = lax.axis_index("ctx") * rows + jnp.arange(rows, dtype=jnp.int32)
    frequencies = 10000.0 ** (-jnp.arange(half_dim, dtype=jnp.float32) / half_dim)
    angles = positions.astype(jnp.float32)[:, None] * frequencies[None, :]
    cosine, sine = jnp.cos(angles), jnp.sin(angles)
    cos_all = jnp.concatenate([cosine, cosine], axis=1)
    sin_all = jnp.concatenate([-sine, sine], axis=1)
    any_spec = pl.BlockSpec(memory_space=pl.ANY)
    vmem_spec = pl.BlockSpec(memory_space=pltpu.VMEM)
    bf16 = jnp.bfloat16
    dma = pltpu.SemaphoreType.DMA
    out = pl.pallas_call(
        functools.partial(layer_kernel, n_ctx, reach, qw // head, kw // head, head),
        out_shape=jax.ShapeDtypeStruct((rows, features), bf16),
        in_specs=[any_spec] * 5 + [vmem_spec] * 6,
        out_specs=vmem_spec,
        scratch_shapes=[
            pltpu.VMEM((rows, features), bf16),
            pltpu.VMEM((features, qw + 2 * kw), bf16),
            pltpu.VMEM((qw, features), bf16),
            pltpu.VMEM((4, rows, features), bf16),
            pltpu.VMEM((rows, qw + 2 * kw), jnp.float32),
            pltpu.VMEM((4, rows, qw), bf16),
            pltpu.VMEM((4, reach + 1, 2, rows, 2 * kw), bf16),
            pltpu.VMEM((4, rows, qw), bf16),
            pltpu.VMEM((4, rows, features), bf16),
            pltpu.VMEM((rows, features), bf16),
            pltpu.VMEM((rows, features), bf16),
            pltpu.VMEM((rows, features), bf16),
            pltpu.VMEM((1, features), jnp.float32),
            pltpu.VMEM((1, features), jnp.float32),
            pltpu.VMEM((2 * kw // head, qw // kw * rows, head), jnp.float32),
            pltpu.VMEM((2 * kw // head, qw // kw * rows, rows), jnp.float32),
            dma((9,)), dma((6,)), dma((6,)), dma((10,)), dma((10,)),
            dma((4, reach + 1)), dma((4, reach + 1)), dma((4, reach + 1)), dma((4, reach + 1)),
        ],
        compiler_params=pltpu.CompilerParams(
            collective_id=0, has_side_effects=True, vmem_limit_bytes=vmem_limit
        ),
    )(
        tokens[0], w_query, key_weight, value_weight, w_out,
        pre_gain.reshape(-1, 128), post_gain.reshape(-1, 128), query_norm_gain[None], key_gain[None], cos_all, sin_all,
    )
    return out[None]


def solution(mesh):
    return jax.shard_map(
        functools.partial(per_device, mesh.shape["ctx"]),
        mesh=mesh,
        in_specs=(
            P("fsdp", "ctx", None),
            P(),
            P(None, "fsdp"),
            P(None, "fsdp"),
            P(None, "fsdp"),
            P(),
            P(),
            P("fsdp", None),
            P(),
        ),
        out_specs=P("fsdp", "ctx", None),
        check_vma=False,
    )
```

```python
import functools
import math

import jax
import jax.numpy as jnp
from jax import lax
from jax.experimental import pallas as pl
from jax.experimental.pallas import tpu as pltpu
from jax.sharding import PartitionSpec as P

epsilon = 1e-06
score_scale = 168.0 ** (-0.5)
window = 1024
vmem_limit = 58_000_000
MESH = pl.DeviceIdType.MESH
halves_of = ((0, 0), (1, 2), (2, 1), (3, 3))


def column_step(total, limit):
    step = 128
    for count in range(1, limit // 128 + 1):
        if total % (count * 128) == 0:
            step = count * 128
    return step


def layer_kernel(
    n_ctx, reach, q_heads, kv_heads, head,
    tok_hbm, wq_hbm, wk_hbm, wv_hbm, wo_hbm, pre_ref, post_ref, qg_ref, kg_ref, cos_ref, sin_ref,
    out_ref,
    tok, w, wo, nb, raw, q, kv, att, pb, rx, ry, dg, pre, post, accs, sums,
    load_sem, ag_s, ag_r, rs_s, rs_r, z_s, z_r, b_s, b_r,
):
    f = lax.axis_index("fsdp")
    c = lax.axis_index("ctx")
    rows, features = tok.shape
    half = rows // 2
    z = c // 2
    p = c % 2
    nz = n_ctx // 2
    x_to = {"fsdp": f + 1 - 2 * (f % 2)}
    y_to = {"fsdp": (f + 2) % 4}
    sib = {"ctx": c + 1 - 2 * p}

    def ahead(step):
        return {"ctx": lax.rem(c + 2 * step, n_ctx)}, z + step < nz

    def behind(step):
        return {"ctx": lax.rem(c + n_ctx - 2 * step, n_ctx)}, z >= step

    direct = [step for step in (1, 3) if step <= reach]
    qw, kw = q_heads * head, kv_heads * head
    group = q_heads // kv_heads

    def load(i, src, dst):
        return pltpu.make_async_copy(src, dst, load_sem.at[i])

    tok_loads = [load(i, tok_hbm.at[pl.ds(i * half, half)], tok.at[pl.ds(i * half, half)]) for i in range(2)]
    for d in tok_loads:
        d.start()
    loads = []
    cut = features // 2
    for j, (src, lo, wide) in enumerate(((wk_hbm, qw, kw), (wv_hbm, qw + kw, kw), (wq_hbm, 0, qw))):
        for part in range(2):
            rs = pl.ds(part * cut, cut)
            loads.append(load(2 + 2 * j + part, src.at[rs], w.at[rs, pl.ds(lo, wide)]))
    wo_load = load(8, wo_hbm, wo)

    barrier = pltpu.get_barrier_semaphore()
    for to in (x_to, y_to, sib):
        pl.semaphore_signal(barrier, inc=1, device_id=to, device_id_type=MESH)

    peers = 3
    for step in direct:
        for to, there in (ahead(step), behind(step)):
            pl.when(there)(functools.partial(
                pl.semaphore_signal, barrier, inc=1, device_id=to, device_id_type=MESH
            ))
        peers = peers + jnp.clip(z - step + 1, 0, 1) + jnp.clip(nz - z - step, 0, 1)

    for wide, gain in ((pre, pre_ref), (post, post_ref)):
        wide[...] = jnp.concatenate([gain[k : k + 1, :] for k in range(gain.shape[0])], axis=1)
    tok_loads[0].wait()

    def norm_rows(i, carry):
        at = pl.ds(pl.multiple_of(i * 16, 16), 16)
        v = tok[at, :].astype(jnp.float32)
        mean_sq = jnp.mean(v * v, axis=-1, keepdims=True)
        nb[0, at, :] = (v * lax.rsqrt(mean_sq + epsilon) * pre[...]).astype(jnp.bfloat16)
        return carry

    lax.fori_loop(0, half // 16, norm_rows, 0)
    tok_loads[1].wait()
    for d in loads:
        d.start()
    wo_load.start()
    pl.semaphore_wait(barrier, peers)

    A, B = pl.ds(0, half), pl.ds(half, half)

    def remote(src, dst, s, r, to):
        return pltpu.make_async_remote_copy(
            src_ref=src, dst_ref=dst, send_sem=s, recv_sem=r, device_id=to, device_id_type=MESH
        )

    def ag(i):
        src, dst, to = (
            (nb.at[0, A], nb.at[1, A], x_to),
            (nb.at[0, B], nb.at[2, B], x_to),
            (nb.at[0, B], nb.at[1, B], y_to),
            (nb.at[0, A], nb.at[2, A], y_to),
            (nb.at[1, A], nb.at[3, A], y_to),
            (nb.at[1, B], nb.at[3, B], x_to),
        )[i]
        return remote(src, dst, ag_s.at[i], ag_r.at[i], to)

    ag(0).start()
    lax.fori_loop(half // 16, rows // 16, norm_rows, 0)
    for i in (2, 1, 3):
        ag(i).start()

    def z_copy(u, dz, step):
        return remote(
            kv.at[u, dz, p], kv.at[u, dz + step, p], z_s.at[u, dz + step], z_r.at[u, dz + step], ahead(step)[0]
        )

    def b_copy(u, dz):
        return remote(kv.at[u, dz, p], kv.at[u, dz, p], b_s.at[u, dz], b_r.at[u, dz], sib)

    def kv_arrived(u, dz):
        return remote(kv.at[u, dz, p], kv.at[u, dz, p], z_s.at[u, dz], z_r.at[u, dz], behind(1)[0])

    def kv_paired(u, dz):
        return remote(kv.at[u, dz, 1 - p], kv.at[u, dz, 1 - p], b_s.at[u, dz], b_r.at[u, dz], sib)

    def own_copies(u, act):
        for step in direct:
            @pl.when(ahead(step)[1])
            def _():
                act(z_copy(u, 0, step))

        @pl.when(p == 0)
        def _():
            act(b_copy(u, 0))

    def send_own(u):
        own_copies(u, lambda d: d.start())

    def passed_copies(u, dz, act):
        if dz in direct and dz + 1 <= reach:
            @pl.when(ahead(1)[1])
            def _():
                act(z_copy(u, dz, 1))

        act(b_copy(u, dz))

    def relay(u, dz):
        if dz > reach:
            return

        @pl.when(z >= dz)
        def _():
            kv_arrived(u, dz).wait_recv()
            passed_copies(u, dz, lambda d: d.start())

    def wait_pairs(u):
        @pl.when(p == 1)
        def _():
            kv_paired(u, 0).wait_recv()

        for dz in range(1, reach + 1):
            @pl.when(z >= dz)
            def _():
                kv_paired(u, dz).wait_recv()

    k_step = column_step(2 * kw, 256)
    q_step = column_step(qw, 256)

    def columns_of(u, first, count, step):
        def columns(j, carry):
            at = pl.ds(pl.multiple_of(first + j * step, 128), step)
            raw[:, at] = jnp.dot(nb[u], w[:, at], preferred_element_type=jnp.float32)
            return carry

        lax.fori_loop(0, count // step, columns, 0)

    def rotated(col, gain):
        v = raw[:, col : col + head]
        mean_sq = jnp.mean(v * v, axis=-1, keepdims=True)
        v = v * lax.rsqrt(mean_sq + epsilon) * gain[...]
        return (v * cos_ref[...] + pltpu.roll(v, head // 2, 1) * sin_ref[...]).astype(jnp.bfloat16)

    def project_keys(u):
        columns_of(u, qw, 2 * kw, k_step)
        for h in range(kv_heads):
            kv[u, 0, p, :, h * head : (h + 1) * head] = rotated(qw + h * head, kg_ref)
        kv[u, 0, p, :, kw:] = raw[:, qw + kw :].astype(jnp.bfloat16)

    def project_queries(u):
        columns_of(u, 0, qw, q_step)
        for h in range(q_heads):
            q[u, :, h * head : (h + 1) * head] = rotated(h * head, qg_ref)

    def merged(parts):
        return jnp.concatenate(parts, axis=0)

    def attend(u):
        own, other = halves_of[u], halves_of[(0, 2, 1, 3)[u]]
        spans = [(0, rows, own)] if own == other else [(0, half, own), (half, half, other)]
        streams = [
            (i * kv_heads + g, g, lo, size, units)
            for i, (lo, size, units) in enumerate(spans) for g in range(kv_heads)
        ]

        def places(lo, size):
            qi = lax.broadcasted_iota(jnp.int32, (group, size, rows), 1).reshape(group * size, rows) + lo
            return qi, lax.broadcasted_iota(jnp.int32, (group * size, rows), 1)

        def block(units, dz, par, cols):
            ua, ub = units
            if ua == ub:
                return kv[ua, dz, par, :, cols]
            return merged([kv[ua, dz, par, :half, cols], kv[ub, dz, par, half:, cols]])

        def step(dz, pars, mask, first=False):
            for n, g, lo, size, units in streams:
                kc = slice(g * head, (g + 1) * head)
                vc = slice(kw + g * head, kw + (g + 1) * head)
                at = slice(0, group * size)
                queries = merged([
                    q[u, lo : lo + size, h * head : (h + 1) * head] for h in range(g * group, (g + 1) * group)
                ])
                keys = merged([block(units, dz, par, kc) for par in pars])
                values = merged([block(units, dz, par, vc) for par in pars])
                s = lax.dot_general(queries, keys, (((1,), (1,)), ((), ())), preferred_element_type=jnp.float32)
                e = jnp.exp(s * score_scale)
                if mask is not None:
                    e = jnp.where(mask(lo, size), e, 0.0)
                total = sum(e[:, i * rows : (i + 1) * rows] for i in range(len(pars)))
                acc = jnp.dot(e.astype(jnp.bfloat16), values, preferred_element_type=jnp.float32)
                if first:
                    sums[n, at], accs[n, at] = total, acc
                else:
                    sums[n, at] += total
                    accs[n, at] += acc

        def causal(lo, size):
            qi, kj = places(lo, size)
            return kj <= qi

        step(0, [p], causal, True)

        def beside(_, carry):
            step(0, [0], None)
            return carry

        def earlier(dz, carry):
            def near(lo, size):
                qi, kj = places(lo, size)
                apart = (p + 2 * dz) * rows + qi - kj
                return jnp.concatenate([apart, apart - rows], axis=1) < window

            step(dz, [0, 1], near if n_ctx * rows > window else None)
            return carry

        lax.fori_loop(0, p, beside, 0)
        lax.fori_loop(1, jnp.minimum(z, reach) + 1, earlier, 0)
        for n, g, lo, size, _ in streams:
            at = slice(0, group * size)
            o = (accs[n, at] / jnp.sum(sums[n, at], axis=-1, keepdims=True)).astype(jnp.bfloat16)
            for i in range(group):
                h = g * group + i
                att[u, lo : lo + size, h * head : (h + 1) * head] = o[i * size : (i + 1) * size]

    o_step = column_step(features, 768)

    def output(u):
        def columns(j, carry):
            at = pl.ds(pl.multiple_of(j * o_step, o_step), o_step)
            pb[u, :, at] = jnp.dot(att[u], wo[:, at], preferred_element_type=jnp.float32).astype(jnp.bfloat16)
            return carry

        lax.fori_loop(0, features // o_step, columns, 0)

    quarter = half // 2
    A0, A1 = pl.ds(0, quarter), pl.ds(quarter, quarter)
    B0, B1 = pl.ds(half, quarter), pl.ds(half + quarter, quarter)

    def rs(i):
        src, dst, to = (
            (pb.at[1, A], rx.at[A], x_to),
            (pb.at[1, B], ry.at[B], y_to),
            (pb.at[3, A0], dg.at[A0], x_to),
            (pb.at[3, B0], dg.at[B0], y_to),
            (pb.at[3, A1], dg.at[A1], x_to),
            (pb.at[3, B1], dg.at[B1], y_to),
            (pb.at[2, A0], ry.at[A0], y_to),
            (pb.at[2, B0], rx.at[B0], x_to),
            (pb.at[2, A1], ry.at[A1], y_to),
            (pb.at[2, B1], rx.at[B1], x_to),
        )[i]
        return remote(src, dst, rs_s.at[i], rs_r.at[i], to)

    for d in loads:
        d.wait()
    project_keys(0)
    ag(0).wait_recv()
    ag(4).start()
    ag(2).wait_recv()
    ag(5).start()
    project_keys(1)
    send_own(1)
    project_queries(1)
    relay(1, 1)
    project_queries(0)
    ag(1).wait_recv()
    ag(3).wait_recv()
    project_keys(2)
    send_own(2)
    for dz in range(2, reach + 1):
        relay(1, dz)
    project_queries(2)
    relay(2, 1)
    ag(4).wait_recv()
    ag(5).wait_recv()
    project_keys(3)
    send_own(3)
    for dz in range(2, reach + 1):
        relay(2, dz)
    wo_load.wait()
    wait_pairs(1)
    wait_pairs(2)
    attend(1)
    output(1)
    rs(0).start()
    rs(1).start()
    relay(3, 1)
    attend(2)
    project_queries(3)
    for dz in range(2, reach + 1):
        relay(3, dz)
    send_own(0)
    wait_pairs(3)
    attend(3)
    output(3)
    for i in (2, 3, 4, 5):
        rs(i).start()
    output(2)
    relay(0, 1)

    def add_rows(first, count):
        def body(i, carry):
            at = pl.ds(pl.multiple_of(first + i * 16, 16), 16)
            pb[2, at, :] = (pb[2, at, :].astype(jnp.float32) + dg[at, :].astype(jnp.float32)).astype(jnp.bfloat16)
            return carry

        lax.fori_loop(0, count // 16, body, 0)

    for i, first in ((2, 0), (3, half), (4, quarter), (5, half + quarter)):
        rs(i).wait_recv()
        add_rows(first, quarter)
        rs(i + 4).start()
    for dz in range(2, reach + 1):
        relay(0, dz)
    wait_pairs(0)
    attend(0)
    output(0)

    def finish(first, count):
        def body(i, carry):
            at = pl.ds(pl.multiple_of(first + i * 16, 16), 16)
            summed = pb[0, at, :].astype(jnp.float32) + rx[at, :].astype(jnp.float32) + ry[at, :].astype(jnp.float32)
            mean_sq = jnp.mean(summed * summed, axis=-1, keepdims=True)
            normed = summed * lax.rsqrt(mean_sq + epsilon) * post[...]
            out_ref[at, :] = (tok[at, :].astype(jnp.float32) + normed).astype(jnp.bfloat16)
            return carry

        lax.fori_loop(0, count // 16, body, 0)

    rs(0).wait_recv()
    rs(1).wait_recv()
    for i, first in ((6, 0), (7, half), (8, quarter), (9, half + quarter)):
        rs(i).wait_recv()
        finish(first, quarter)

    for i in range(6):
        ag(i).wait_send()
    for i in range(10):
        rs(i).wait_send()
    for u in range(4):
        own_copies(u, lambda d: d.wait_send())
        for dz in range(1, reach + 1):
            @pl.when(z >= dz)
            def _():
                passed_copies(u, dz, lambda d: d.wait_send())


def per_device(
    n_ctx, tokens, pre_gain, w_query, key_weight, value_weight, query_norm_gain, key_gain, w_out, post_gain
):
    _, rows, features = tokens.shape
    head = query_norm_gain.shape[0]
    qw, kw = w_query.shape[1], key_weight.shape[1]
    reach = min(n_ctx // 2 - 1, -(-window // (2 * rows)))
    half_dim = head // 2
    positions = lax.axis_index("ctx") * rows + jnp.arange(rows, dtype=jnp.int32)
    frequencies = 10000.0 ** (-jnp.arange(half_dim, dtype=jnp.float32) / half_dim)
    angles = positions.astype(jnp.float32)[:, None] * frequencies[None, :]
    cosine, sine = jnp.cos(angles), jnp.sin(angles)
    cos_all = jnp.concatenate([cosine, cosine], axis=1)
    sin_all = jnp.concatenate([-sine, sine], axis=1)
    any_spec = pl.BlockSpec(memory_space=pl.ANY)
    vmem_spec = pl.BlockSpec(memory_space=pltpu.VMEM)
    bf16 = jnp.bfloat16
    dma = pltpu.SemaphoreType.DMA
    out = pl.pallas_call(
        functools.partial(layer_kernel, n_ctx, reach, qw // head, kw // head, head),
        out_shape=jax.ShapeDtypeStruct((rows, features), bf16),
        in_specs=[any_spec] * 5 + [vmem_spec] * 6,
        out_specs=vmem_spec,
        scratch_shapes=[
            pltpu.VMEM((rows, features), bf16),
            pltpu.VMEM((features, qw + 2 * kw), bf16),
            pltpu.VMEM((qw, features), bf16),
            pltpu.VMEM((4, rows, features), bf16),
            pltpu.VMEM((rows, qw + 2 * kw), jnp.float32),
            pltpu.VMEM((4, rows, qw), bf16),
            pltpu.VMEM((4, reach + 1, 2, rows, 2 * kw), bf16),
            pltpu.VMEM((4, rows, qw), bf16),
            pltpu.VMEM((4, rows, features), bf16),
            pltpu.VMEM((rows, features), bf16),
            pltpu.VMEM((rows, features), bf16),
            pltpu.VMEM((rows, features), bf16),
            pltpu.VMEM((1, features), jnp.float32),
            pltpu.VMEM((1, features), jnp.float32),
            pltpu.VMEM((2 * kw // head, qw // kw * rows, head), jnp.float32),
            pltpu.VMEM((2 * kw // head, qw // kw * rows, rows), jnp.float32),
            dma((9,)), dma((6,)), dma((6,)), dma((10,)), dma((10,)),
            dma((4, reach + 1)), dma((4, reach + 1)), dma((4, reach + 1)), dma((4, reach + 1)),
        ],
        compiler_params=pltpu.CompilerParams(
            collective_id=0, has_side_effects=True, vmem_limit_bytes=vmem_limit
        ),
    )(
        tokens[0], w_query, key_weight, value_weight, w_out,
        pre_gain.reshape(-1, 128), post_gain.reshape(-1, 128), query_norm_gain[None], key_gain[None], cos_all, sin_all,
    )
    return out[None]


def solution(mesh):
    return jax.shard_map(
        functools.partial(per_device, mesh.shape["ctx"]),
        mesh=mesh,
        in_specs=(
            P("fsdp", "ctx", None),
            P(),
            P(None, "fsdp"),
            P(None, "fsdp"),
            P(None, "fsdp"),
            P(),
            P(),
            P("fsdp", None),
            P(),
        ),
        out_specs=P("fsdp", "ctx", None),
        check_vma=False,
    )
```

```python
import functools
import math

import jax
import jax.numpy as jnp
from jax import lax
from jax.experimental import pallas as pl
from jax.experimental.pallas import tpu as pltpu
from jax.sharding import PartitionSpec as P

epsilon = 1e-06
score_scale = 168.0 ** (-0.5)
window = 1024
vmem_limit = 58_000_000
MESH = pl.DeviceIdType.MESH
halves_of = ((0, 0), (1, 2), (2, 1), (3, 3))


def column_step(total, limit):
    step = 128
    for count in range(1, limit // 128 + 1):
        if total % (count * 128) == 0:
            step = count * 128
    return step


def layer_kernel(
    n_ctx, reach, q_heads, kv_heads, head,
    tok_hbm, wq_hbm, wk_hbm, wv_hbm, wo_hbm, pre_ref, post_ref, qg_ref, kg_ref, cos_ref, sin_ref,
    out_ref,
    tok, w, wo, nb, raw, q, kv, att, pb, rx, ry, dg, pre, post, accs, sums,
    load_sem, ag_s, ag_r, rs_s, rs_r, z_s, z_r, b_s, b_r,
):
    f = lax.axis_index("fsdp")
    c = lax.axis_index("ctx")
    rows, features = tok.shape
    half = rows // 2
    z = c // 2
    p = c % 2
    nz = n_ctx // 2
    x_to = {"fsdp": f + 1 - 2 * (f % 2)}
    y_to = {"fsdp": (f + 2) % 4}
    sib = {"ctx": c + 1 - 2 * p}

    def ahead(step):
        return {"ctx": lax.rem(c + 2 * step, n_ctx)}, z + step < nz

    def behind(step):
        return {"ctx": lax.rem(c + n_ctx - 2 * step, n_ctx)}, z >= step

    direct = [step for step in (1, 3) if step <= reach]
    qw, kw = q_heads * head, kv_heads * head
    group = q_heads // kv_heads

    def load(i, src, dst):
        return pltpu.make_async_copy(src, dst, load_sem.at[i])

    tok_loads = [load(i, tok_hbm.at[pl.ds(i * half, half)], tok.at[pl.ds(i * half, half)]) for i in range(2)]
    for d in tok_loads:
        d.start()
    loads = []
    cut = features // 2
    for j, (src, lo, wide) in enumerate(((wk_hbm, qw, kw), (wv_hbm, qw + kw, kw), (wq_hbm, 0, qw))):
        for part in range(2):
            rs = pl.ds(part * cut, cut)
            loads.append(load(2 + 2 * j + part, src.at[rs], w.at[rs, pl.ds(lo, wide)]))
    wo_load = load(8, wo_hbm, wo)

    barrier = pltpu.get_barrier_semaphore()
    for to in (x_to, y_to, sib):
        pl.semaphore_signal(barrier, inc=1, device_id=to, device_id_type=MESH)

    peers = 3
    for step in direct:
        for to, there in (ahead(step), behind(step)):
            pl.when(there)(functools.partial(
                pl.semaphore_signal, barrier, inc=1, device_id=to, device_id_type=MESH
            ))
        peers = peers + jnp.clip(z - step + 1, 0, 1) + jnp.clip(nz - z - step, 0, 1)

    for wide, gain in ((pre, pre_ref), (post, post_ref)):
        wide[...] = jnp.concatenate([gain[k : k + 1, :] for k in range(gain.shape[0])], axis=1)
    tok_loads[0].wait()

    def norm_rows(i, carry):
        at = pl.ds(pl.multiple_of(i * 16, 16), 16)
        v = tok[at, :].astype(jnp.float32)
        mean_sq = jnp.mean(v * v, axis=-1, keepdims=True)
        nb[0, at, :] = (v * lax.rsqrt(mean_sq + epsilon) * pre[...]).astype(jnp.bfloat16)
        return carry

    lax.fori_loop(0, half // 16, norm_rows, 0)
    tok_loads[1].wait()
    for d in loads:
        d.start()
    wo_load.start()
    pl.semaphore_wait(barrier, peers)

    A, B = pl.ds(0, half), pl.ds(half, half)

    def remote(src, dst, s, r, to):
        return pltpu.make_async_remote_copy(
            src_ref=src, dst_ref=dst, send_sem=s, recv_sem=r, device_id=to, device_id_type=MESH
        )

    def ag(i):
        src, dst, to = (
            (nb.at[0, A], nb.at[1, A], x_to),
            (nb.at[0, B], nb.at[2, B], x_to),
            (nb.at[0, B], nb.at[1, B], y_to),
            (nb.at[0, A], nb.at[2, A], y_to),
            (nb.at[1, A], nb.at[3, A], y_to),
            (nb.at[1, B], nb.at[3, B], x_to),
        )[i]
        return remote(src, dst, ag_s.at[i], ag_r.at[i], to)

    ag(0).start()
    lax.fori_loop(half // 16, rows // 16, norm_rows, 0)
    for i in (2, 1, 3):
        ag(i).start()

    def z_copy(u, dz, step):
        return remote(
            kv.at[u, dz, p], kv.at[u, dz + step, p], z_s.at[u, dz + step], z_r.at[u, dz + step], ahead(step)[0]
        )

    def b_copy(u, dz):
        return remote(kv.at[u, dz, p], kv.at[u, dz, p], b_s.at[u, dz], b_r.at[u, dz], sib)

    def kv_arrived(u, dz):
        return remote(kv.at[u, dz, p], kv.at[u, dz, p], z_s.at[u, dz], z_r.at[u, dz], behind(1)[0])

    def kv_paired(u, dz):
        return remote(kv.at[u, dz, 1 - p], kv.at[u, dz, 1 - p], b_s.at[u, dz], b_r.at[u, dz], sib)

    def own_copies(u, act):
        for step in direct:
            @pl.when(ahead(step)[1])
            def _():
                act(z_copy(u, 0, step))

        @pl.when(p == 0)
        def _():
            act(b_copy(u, 0))

    def send_own(u):
        own_copies(u, lambda d: d.start())

    def passed_copies(u, dz, act):
        if dz in direct and dz + 1 <= reach:
            @pl.when(ahead(1)[1])
            def _():
                act(z_copy(u, dz, 1))

        act(b_copy(u, dz))

    def relay(u, dz):
        if dz > reach:
            return

        @pl.when(z >= dz)
        def _():
            kv_arrived(u, dz).wait_recv()
            passed_copies(u, dz, lambda d: d.start())

    def wait_pairs(u):
        @pl.when(p == 1)
        def _():
            kv_paired(u, 0).wait_recv()

        for dz in range(1, reach + 1):
            @pl.when(z >= dz)
            def _():
                kv_paired(u, dz).wait_recv()

    k_step = column_step(2 * kw, 256)
    q_step = column_step(qw, 256)

    def columns_of(u, first, count, step):
        def columns(j, carry):
            at = pl.ds(pl.multiple_of(first + j * step, 128), step)
            raw[:, at] = jnp.dot(nb[u], w[:, at], preferred_element_type=jnp.float32)
            return carry

        lax.fori_loop(0, count // step, columns, 0)

    def rotated(col, gain):
        v = raw[:, col : col + head]
        mean_sq = jnp.mean(v * v, axis=-1, keepdims=True)
        v = v * lax.rsqrt(mean_sq + epsilon) * gain[...]
        return (v * cos_ref[...] + pltpu.roll(v, head // 2, 1) * sin_ref[...]).astype(jnp.bfloat16)

    def project_keys(u):
        columns_of(u, qw, 2 * kw, k_step)
        for h in range(kv_heads):
            kv[u, 0, p, :, h * head : (h + 1) * head] = rotated(qw + h * head, kg_ref)
        kv[u, 0, p, :, kw:] = raw[:, qw + kw :].astype(jnp.bfloat16)

    def project_queries(u):
        columns_of(u, 0, qw, q_step)
        for h in range(q_heads):
            q[u, :, h * head : (h + 1) * head] = rotated(h * head, qg_ref)

    def merged(parts):
        return jnp.concatenate(parts, axis=0)

    def attend(u):
        own, other = halves_of[u], halves_of[(0, 2, 1, 3)[u]]
        spans = [(0, rows, own)] if own == other else [(0, half, own), (half, half, other)]
        streams = [
            (i * kv_heads + g, g, lo, size, units)
            for i, (lo, size, units) in enumerate(spans) for g in range(kv_heads)
        ]

        def places(lo, size):
            qi = lax.broadcasted_iota(jnp.int32, (group, size, rows), 1).reshape(group * size, rows) + lo
            return qi, lax.broadcasted_iota(jnp.int32, (group * size, rows), 1)

        def block(units, dz, par, cols):
            ua, ub = units
            if ua == ub:
                return kv[ua, dz, par, :, cols]
            return merged([kv[ua, dz, par, :half, cols], kv[ub, dz, par, half:, cols]])

        def step(dz, pars, mask, first=False):
            for n, g, lo, size, units in streams:
                kc = slice(g * head, (g + 1) * head)
                vc = slice(kw + g * head, kw + (g + 1) * head)
                at = slice(0, group * size)
                queries = merged([
                    q[u, lo : lo + size, h * head : (h + 1) * head] for h in range(g * group, (g + 1) * group)
                ])
                keys = merged([block(units, dz, par, kc) for par in pars])
                values = merged([block(units, dz, par, vc) for par in pars])
                s = lax.dot_general(queries, keys, (((1,), (1,)), ((), ())), preferred_element_type=jnp.float32)
                e = jnp.exp(s * score_scale)
                if mask is not None:
                    e = jnp.where(mask(lo, size), e, 0.0)
                total = sum(e[:, i * rows : (i + 1) * rows] for i in range(len(pars)))
                acc = jnp.dot(e.astype(jnp.bfloat16), values, preferred_element_type=jnp.float32)
                if first:
                    sums[n, at], accs[n, at] = total, acc
                else:
                    sums[n, at] += total
                    accs[n, at] += acc

        def causal(lo, size):
            qi, kj = places(lo, size)
            return kj <= qi

        step(0, [p], causal, True)

        def beside(_, carry):
            step(0, [0], None)
            return carry

        def earlier(dz, carry):
            def near(lo, size):
                qi, kj = places(lo, size)
                apart = (p + 2 * dz) * rows + qi - kj
                return jnp.concatenate([apart, apart - rows], axis=1) < window

            step(dz, [0, 1], near if n_ctx * rows > window else None)
            return carry

        lax.fori_loop(0, p, beside, 0)
        lax.fori_loop(1, jnp.minimum(z, reach) + 1, earlier, 0)
        for n, g, lo, size, _ in streams:
            at = slice(0, group * size)
            o = (accs[n, at] / jnp.sum(sums[n, at], axis=-1, keepdims=True)).astype(jnp.bfloat16)
            for i in range(group):
                h = g * group + i
                att[u, lo : lo + size, h * head : (h + 1) * head] = o[i * size : (i + 1) * size]

    o_step = column_step(features, 768)

    def output(u):
        def columns(j, carry):
            at = pl.ds(pl.multiple_of(j * o_step, o_step), o_step)
            pb[u, :, at] = jnp.dot(att[u], wo[:, at], preferred_element_type=jnp.float32).astype(jnp.bfloat16)
            return carry

        lax.fori_loop(0, features // o_step, columns, 0)

    quarter = half // 2
    A0, A1 = pl.ds(0, quarter), pl.ds(quarter, quarter)
    B0, B1 = pl.ds(half, quarter), pl.ds(half + quarter, quarter)

    def rs(i):
        src, dst, to = (
            (pb.at[1, A], rx.at[A], x_to),
            (pb.at[1, B], ry.at[B], y_to),
            (pb.at[3, A0], dg.at[A0], x_to),
            (pb.at[3, B0], dg.at[B0], y_to),
            (pb.at[3, A1], dg.at[A1], x_to),
            (pb.at[3, B1], dg.at[B1], y_to),
            (pb.at[2, A0], ry.at[A0], y_to),
            (pb.at[2, B0], rx.at[B0], x_to),
            (pb.at[2, A1], ry.at[A1], y_to),
            (pb.at[2, B1], rx.at[B1], x_to),
        )[i]
        return remote(src, dst, rs_s.at[i], rs_r.at[i], to)

    for d in loads:
        d.wait()
    project_keys(0)
    ag(0).wait_recv()
    ag(4).start()
    ag(2).wait_recv()
    ag(5).start()
    project_keys(1)
    send_own(1)
    project_queries(1)
    relay(1, 1)
    project_queries(0)
    ag(1).wait_recv()
    ag(3).wait_recv()
    project_keys(2)
    send_own(2)
    for dz in range(2, reach + 1):
        relay(1, dz)
    project_queries(2)
    relay(2, 1)
    relay(2, 2)
    ag(4).wait_recv()
    ag(5).wait_recv()
    project_keys(3)
    send_own(3)
    for dz in range(3, reach + 1):
        relay(2, dz)
    wo_load.wait()
    wait_pairs(1)
    wait_pairs(2)
    attend(1)
    output(1)
    rs(0).start()
    rs(1).start()
    relay(3, 1)
    attend(2)
    project_queries(3)
    for dz in range(2, reach + 1):
        relay(3, dz)
    send_own(0)
    wait_pairs(3)
    attend(3)
    output(3)
    for i in (2, 3, 4, 5):
        rs(i).start()
    output(2)
    relay(0, 1)

    def add_rows(first, count):
        def body(i, carry):
            at = pl.ds(pl.multiple_of(first + i * 16, 16), 16)
            pb[2, at, :] = (pb[2, at, :].astype(jnp.float32) + dg[at, :].astype(jnp.float32)).astype(jnp.bfloat16)
            return carry

        lax.fori_loop(0, count // 16, body, 0)

    for i, first in ((2, 0), (3, half), (4, quarter), (5, half + quarter)):
        rs(i).wait_recv()
        add_rows(first, quarter)
        rs(i + 4).start()
    for dz in range(2, reach + 1):
        relay(0, dz)
    wait_pairs(0)
    attend(0)
    output(0)

    def finish(first, count):
        def body(i, carry):
            at = pl.ds(pl.multiple_of(first + i * 16, 16), 16)
            summed = pb[0, at, :].astype(jnp.float32) + rx[at, :].astype(jnp.float32) + ry[at, :].astype(jnp.float32)
            mean_sq = jnp.mean(summed * summed, axis=-1, keepdims=True)
            normed = summed * lax.rsqrt(mean_sq + epsilon) * post[...]
            out_ref[at, :] = (tok[at, :].astype(jnp.float32) + normed).astype(jnp.bfloat16)
            return carry

        lax.fori_loop(0, count // 16, body, 0)

    rs(0).wait_recv()
    rs(1).wait_recv()
    for i, first in ((6, 0), (7, half), (8, quarter), (9, half + quarter)):
        rs(i).wait_recv()
        finish(first, quarter)

    for i in range(6):
        ag(i).wait_send()
    for i in range(10):
        rs(i).wait_send()
    for u in range(4):
        own_copies(u, lambda d: d.wait_send())
        for dz in range(1, reach + 1):
            @pl.when(z >= dz)
            def _():
                passed_copies(u, dz, lambda d: d.wait_send())


def per_device(
    n_ctx, tokens, pre_gain, w_query, key_weight, value_weight, query_norm_gain, key_gain, w_out, post_gain
):
    _, rows, features = tokens.shape
    head = query_norm_gain.shape[0]
    qw, kw = w_query.shape[1], key_weight.shape[1]
    reach = min(n_ctx // 2 - 1, -(-window // (2 * rows)))
    half_dim = head // 2
    positions = lax.axis_index("ctx") * rows + jnp.arange(rows, dtype=jnp.int32)
    frequencies = 10000.0 ** (-jnp.arange(half_dim, dtype=jnp.float32) / half_dim)
    angles = positions.astype(jnp.float32)[:, None] * frequencies[None, :]
    cosine, sine = jnp.cos(angles), jnp.sin(angles)
    cos_all = jnp.concatenate([cosine, cosine], axis=1)
    sin_all = jnp.concatenate([-sine, sine], axis=1)
    any_spec = pl.BlockSpec(memory_space=pl.ANY)
    vmem_spec = pl.BlockSpec(memory_space=pltpu.VMEM)
    bf16 = jnp.bfloat16
    dma = pltpu.SemaphoreType.DMA
    out = pl.pallas_call(
        functools.partial(layer_kernel, n_ctx, reach, qw // head, kw // head, head),
        out_shape=jax.ShapeDtypeStruct((rows, features), bf16),
        in_specs=[any_spec] * 5 + [vmem_spec] * 6,
        out_specs=vmem_spec,
        scratch_shapes=[
            pltpu.VMEM((rows, features), bf16),
            pltpu.VMEM((features, qw + 2 * kw), bf16),
            pltpu.VMEM((qw, features), bf16),
            pltpu.VMEM((4, rows, features), bf16),
            pltpu.VMEM((rows, qw + 2 * kw), jnp.float32),
            pltpu.VMEM((4, rows, qw), bf16),
            pltpu.VMEM((4, reach + 1, 2, rows, 2 * kw), bf16),
            pltpu.VMEM((4, rows, qw), bf16),
            pltpu.VMEM((4, rows, features), bf16),
            pltpu.VMEM((rows, features), bf16),
            pltpu.VMEM((rows, features), bf16),
            pltpu.VMEM((rows, features), bf16),
            pltpu.VMEM((1, features), jnp.float32),
            pltpu.VMEM((1, features), jnp.float32),
            pltpu.VMEM((2 * kw // head, qw // kw * rows, head), jnp.float32),
            pltpu.VMEM((2 * kw // head, qw // kw * rows, rows), jnp.float32),
            dma((9,)), dma((6,)), dma((6,)), dma((10,)), dma((10,)),
            dma((4, reach + 1)), dma((4, reach + 1)), dma((4, reach + 1)), dma((4, reach + 1)),
        ],
        compiler_params=pltpu.CompilerParams(
            collective_id=0, has_side_effects=True, vmem_limit_bytes=vmem_limit
        ),
    )(
        tokens[0], w_query, key_weight, value_weight, w_out,
        pre_gain.reshape(-1, 128), post_gain.reshape(-1, 128), query_norm_gain[None], key_gain[None], cos_all, sin_all,
    )
    return out[None]


def solution(mesh):
    return jax.shard_map(
        functools.partial(per_device, mesh.shape["ctx"]),
        mesh=mesh,
        in_specs=(
            P("fsdp", "ctx", None),
            P(),
            P(None, "fsdp"),
            P(None, "fsdp"),
            P(None, "fsdp"),
            P(),
            P(),
            P("fsdp", None),
            P(),
        ),
        out_specs=P("fsdp", "ctx", None),
        check_vma=False,
    )
```
